512 devices in a mesh: beam: 16 (over z, x_hi), tile: 32 (over y, x_lo, core).
Axes of the slice: x: 4 (x_hi: 2, x_lo: 2; x = x_hi * 2 + x_lo), y: 8, z: 8, core: 2. Of those that a mesh axis runs over, the one named last changes fastest.
Arguments:
- scattering: float32 [64, 2, 4096, 256], P('beam', None, 'tile'), may hold values from -4 to 4
- potential: float32 [4096, 256], P('tile'), may hold values from -6 to 6
- row_offset: int32 [16, 32], P(None, 'tile'), may hold values from 0 to 64
- col_offset: int32 [16, 32], P(None, 'tile'), may hold values from 0 to 128
- table_index: int32 [16, 32], P(None, 'tile'), may hold values from 0 to 3
- beam_tilt: int32 [2, 64], P(None, 'beam'), may hold values from -8 to 8
- coef_table: float32 [2, 4, 64], P(None, None, 'beam'), may hold values from -0.75 to 0.75
- measured: float32 [16, 32, 128, 128], P(None, 'tile'), may hold values from 0 to 2
Outputs:
- residual: float32 [16, 32, 128, 128], P('beam', 'tile')
- gradient: float32 [4096, 256], P('tile')
The draws below stay inside these ranges and needn't reach their ends.
All inputs are finite; a program needn't handle non-finite values.
Results may differ from the reference program's by a relative error of at most 0.0002.
Values sent between devices are 32-bit elements; how exact they have to be, the bound alone decides.
No kernel may reach another device: no remote copies, remote signals or barrier semaphores. Data moves between devices by JAX's collectives and lax.ppermute only.
A program may use at most 64 MiB of HBM per device.

```python
import math
import jax
import jax.numpy as jnp
from jax import lax

PATCH = 128
MARGIN = 32
ROWS = 128
COLS = 256
NTAB = 4
BEAMS = 64
P_TILE = 16
NR = 4096
N_TILE = 32


def set_ends(values, key, least, high):
    longest = values.shape.index(max(values.shape))
    spots = []
    for shift in (0, 1):
        where = [jax.random.randint(jax.random.fold_in(key, axis), (), 0, length) for axis, length in enumerate(values.shape)]
        where[longest] = (where[longest] + shift) % values.shape[longest]
        spots.append(tuple(where))
    return values.at[spots[0]].set(least).at[spots[1]].set(high)


def shard_levels(stream_key, extent, cuts, least, top_value):
    loudness, own = 1.0, jax.random.fold_in(stream_key, 6)
    for axis_at, blocks in cuts:
        draws = jnp.exp(jax.random.uniform(jax.random.fold_in(own, axis_at), (blocks,), jnp.float32, least / len(cuts), top_value / len(cuts)))
        loudness = loudness * jnp.repeat(draws, extent[axis_at] // blocks).reshape([-1 if axis == axis_at else 1 for axis in range(len(extent))])
    return loudness


def bell_draw(stream_key, extent, width, reach, cuts=(), held_as=jnp.bfloat16):
    result = jax.random.normal(stream_key, extent, jnp.float32) * width
    if len(cuts) > 0:
        result = shard_levels(stream_key, extent, cuts, -0.22, 0.18) * result
    return jnp.clip(result, min=-reach, max=reach).astype(held_as)


def setup_inputs(seed: int = 0) -> dict:
    keys = jax.random.split(jax.random.key(seed), 9)
    return {
        "scattering": bell_draw(keys[0], (BEAMS, 2, NR, COLS), 0.5, 4.0, ((0, 16), (2, 32)), jnp.float32),
        "potential": bell_draw(keys[1], (NR, COLS), 1.0, 6.0, ((0, 32),), jnp.float32),
        "row_offset": set_ends(jax.random.randint(keys[2], (P_TILE, N_TILE), 0, 2 * MARGIN + 1), jax.random.fold_in(keys[2], 1), 0, 2 * MARGIN).astype(jnp.int32),
        "col_offset": set_ends(jax.random.randint(keys[3], (P_TILE, N_TILE), 0, COLS - PATCH + 1), jax.random.fold_in(keys[3], 1), 0, COLS - PATCH).astype(jnp.int32),
        "table_index": set_ends(jax.random.randint(keys[4], (P_TILE, N_TILE), 0, NTAB), jax.random.fold_in(keys[4], 1), 0, NTAB - 1).astype(jnp.int32),
        "beam_tilt": set_ends(jax.random.randint(keys[5], (2, BEAMS), -8, 9), jax.random.fold_in(keys[5], 1), -8, 8).astype(jnp.int32),
        "coef_table": bell_draw(keys[6], (2, NTAB, BEAMS), BEAMS ** -0.5, 0.75, ((2, 16),), jnp.float32),
        "measured": jnp.clip(2.0 * jax.random.uniform(keys[7], (P_TILE, N_TILE, PATCH, PATCH), jnp.float32) ** shard_levels(keys[7], (P_TILE, N_TILE, PATCH, PATCH), ((1, 32),), -0.2, 0.2), 0.0, 2.0),
    }


SIGMA_SCALE = 1.0
HIGH = lax.Precision.HIGHEST

def dft_parts(inverse):
    pixel_index = jnp.arange(PATCH, dtype=jnp.int32)
    phase_turns = (pixel_index[:, None] * pixel_index[None, :] % PATCH).astype(jnp.float32)
    dft_angle = phase_turns * (2.0 * math.pi / PATCH)
    unit_scale = 1.0 / math.sqrt(PATCH)
    sin_sign = 1.0 if inverse else -1.0
    return (jnp.cos(dft_angle) * unit_scale, sin_sign * jnp.sin(dft_angle) * unit_scale)

def complex_dot(left_re, left_im, right_re, right_im):
    part_re = jnp.dot(left_re, right_re, precision=HIGH) - jnp.dot(left_im, right_im, precision=HIGH)
    part_im = jnp.dot(left_re, right_im, precision=HIGH) + jnp.dot(left_im, right_re, precision=HIGH)
    return (part_re, part_im)

def transform(value_re, value_im, table_re, table_im):
    half_re, half_im = complex_dot(table_re, table_im, value_re, value_im)
    return complex_dot(half_re, half_im, table_re, table_im)

def reference(scattering, potential, row_offset, col_offset, table_index, beam_tilt, coef_table, measured):
    wide = jnp.pad(scattering, ((0, 0), (0, 0), (MARGIN, MARGIN), (0, 0)))
    phase_map = jnp.pad(potential, ((MARGIN, MARGIN), (0, 0))) * SIGMA_SCALE
    forward_re, forward_im = dft_parts(False)
    inverse_re, inverse_im = dft_parts(True)
    tile_ids = jnp.arange(N_TILE, dtype=jnp.int32)
    start_row = (row_offset + tile_ids[None, :] * ROWS).reshape(-1).astype(jnp.int32)
    start_col = col_offset.reshape(-1).astype(jnp.int32)
    corner_row = start_row - MARGIN
    phase_turns = (beam_tilt[0][None, :] * corner_row[:, None] + beam_tilt[1][None, :] * start_col[:, None]) % PATCH
    tilt_angle = phase_turns.astype(jnp.float32) * (2.0 * math.pi / PATCH)
    picked_re = coef_table[0][table_index.reshape(-1)]
    picked_im = coef_table[1][table_index.reshape(-1)]
    coef_re = picked_re * jnp.cos(tilt_angle) + picked_im * jnp.sin(tilt_angle)
    coef_im = picked_im * jnp.cos(tilt_angle) - picked_re * jnp.sin(tilt_angle)
    observed = measured.reshape(-1, PATCH, PATCH)
    zero_index = jnp.zeros((), jnp.int32)

    def one_position(record):
        row_at, col_at, weight_re, weight_im, seen_here = record
        region = lax.dynamic_slice(wide, (zero_index, zero_index, row_at, col_at), (BEAMS, 2, PATCH, PATCH))
        wave_re = jnp.einsum('b,bij->ij', weight_re, region[:, 0], precision=HIGH) - jnp.einsum('b,bij->ij', weight_im, region[:, 1], precision=HIGH)
        wave_im = jnp.einsum('b,bij->ij', weight_re, region[:, 1], precision=HIGH) + jnp.einsum('b,bij->ij', weight_im, region[:, 0], precision=HIGH)
        local_pot = lax.dynamic_slice(phase_map, (row_at, col_at), (PATCH, PATCH))
        trans_re = jnp.cos(local_pot)
        trans_im = jnp.sin(local_pot)
        exit_re = trans_re * wave_re - trans_im * wave_im
        exit_im = trans_re * wave_im + trans_im * wave_re
        far_re, far_im = transform(exit_re, exit_im, forward_re, forward_im)
        misfit = far_re * far_re + far_im * far_im - seen_here
        back_re, back_im = transform(misfit * far_re, misfit * far_im, inverse_re, inverse_im)
        piece = SIGMA_SCALE * (exit_re * back_im - exit_im * back_re)
        return (misfit, piece)
    misfits, pieces = lax.map(one_position, (start_row, start_col, coef_re, coef_im, observed))

    def add_piece(accum_grid, record):
        row_at, col_at, piece = record
        current = lax.dynamic_slice(accum_grid, (row_at, col_at), (PATCH, PATCH))
        return (lax.dynamic_update_slice(accum_grid, current + piece, (row_at, col_at)), None)
    accum_grid, _ = lax.scan(add_piece, jnp.zeros((NR + 2 * MARGIN, COLS), jnp.float32), (start_row, start_col, pieces))
    residual = misfits.reshape(P_TILE, N_TILE, PATCH, PATCH)
    gradient = accum_grid[MARGIN:MARGIN + NR]
    return (residual, gradient)
```

```python
import math

import jax
import jax.numpy as jnp
import numpy as np
from jax import lax
from jax.experimental import pallas as pl
from jax.experimental.pallas import tpu as pltpu
from jax.sharding import PartitionSpec as P

MARGIN = 32
SIGMA_SCALE = 1.0
LANES = 128
BAND = 8

VMEM = pltpu.MemorySpace.VMEM
SMEM = pltpu.MemorySpace.SMEM


def dft_blocks(length):
    index = np.arange(length)
    angle = (index[:, None] * index[None, :] % length) * (2.0 * math.pi / length)
    re = np.cos(angle) / math.sqrt(length)
    im = -np.sin(angle) / math.sqrt(length)
    forward = np.block([[re, im], [-im, re]]).astype(np.float32)
    parts = []
    for table in (forward, forward.T):
        high = table.astype(jnp.bfloat16)
        parts += [high, (table - high.astype(np.float32)).astype(jnp.bfloat16)]
    return np.stack(parts)


def split(value):
    high = value.astype(jnp.bfloat16)
    return high, (value - high.astype(jnp.float32)).astype(jnp.bfloat16)


def dot3(left, right):
    def dot(a, b):
        return jnp.dot(a, b, preferred_element_type=jnp.float32)

    return dot(left[0], right[0]) + (dot(left[0], right[1]) + dot(left[1], right[0]))


def pack_kernel(me_ref, tilt_ref, table_ref, waves_ref, out_ref, sem):
    planes = waves_ref.shape[0]
    copies = [
        pltpu.make_async_copy(
            waves_ref.at[plane, :, :, pl.ds(half * LANES, LANES)],
            out_ref.at[:, pl.ds((half * planes + plane) * BAND, BAND), :],
            sem.at[half * planes + plane],
        )
        for half in range(2)
        for plane in range(planes)
    ]
    for copy in copies:
        copy.start()
    sub = lax.broadcasted_iota(jnp.int32, (BAND, LANES), 0)
    lane = lax.broadcasted_iota(jnp.int32, (BAND, LANES), 1) - me_ref[0] * planes
    tile = jnp.zeros((BAND, LANES), jnp.float32)
    for beam in range(planes // 2):
        for part in range(2):
            here = lane == 2 * beam + part
            for row in range(4):
                value = table_ref[0, row, beam] if part == 0 else -table_ref[1, row, beam]
                tile = jnp.where(here & (sub == row), value, tile)
            for row in range(2):
                tile = jnp.where(here & (sub == 4 + row), tilt_ref[row, beam].astype(jnp.float32), tile)
    for peer in range(out_ref.shape[0]):
        out_ref[peer, 2 * planes * BAND :, :] = tile
    for copy in copies:
        copy.wait()


def exit_kernel(
    cols_ref, beside_cols_ref, spots_ref, beside_ref, recv_ref, potential_ref, own_ref, out_ref, shift_ref
):
    peers = recv_ref.shape[0]
    extra = recv_ref.shape[1] - BAND
    planes = extra // (2 * BAND)
    count = spots_ref.shape[0]

    table = recv_ref[0, extra:, :]
    for peer in range(1, peers):
        table = table + recv_ref[peer, extra:, :]
    lane = lax.broadcasted_iota(jnp.int32, (BAND, LANES), 1)
    swapped = jnp.where(
        lane % 2 == 0, -pltpu.roll(table, LANES - 1, 1), pltpu.roll(table, 1, 1)
    )
    tilt_row = table[4:5].astype(jnp.int32)
    tilt_col = table[5:6].astype(jnp.int32)

    def coefs(ref):
        row = ref[:, 0:1] - MARGIN
        col = ref[:, 1:2]
        pick = ref[:, 2:3]
        turns = (tilt_row * row + tilt_col * col) & (LANES - 1)
        angle = turns.astype(jnp.float32) * (2.0 * math.pi / LANES)
        u = jnp.zeros((count, LANES), jnp.float32)
        v = jnp.zeros((count, LANES), jnp.float32)
        for n in range(4):
            u = jnp.where(pick == n, table[n : n + 1], u)
            v = jnp.where(pick == n, swapped[n : n + 1], v)
        cosine = jnp.cos(angle)
        sine = jnp.sin(angle)
        return u * cosine + v * sine, v * cosine - u * sine

    weights = split(jnp.concatenate(coefs(spots_ref) + coefs(beside_ref), 0))
    local = potential_ref[...] * SIGMA_SCALE
    trans_re = jnp.cos(local)
    trans_im = jnp.sin(local)

    for half in range(2):
        lanes = slice(half * LANES, (half + 1) * LANES)
        for row in range(BAND):
            waves = jnp.concatenate(
                [
                    recv_ref[peer, pl.ds(half * planes * BAND + row, planes, stride=BAND), :]
                    for peer in range(peers)
                ],
                0,
            )
            summed = dot3(weights, split(waves))
            t_re = trans_re[row : row + 1, lanes]
            t_im = trans_im[row : row + 1, lanes]
            for side in range(2):
                w_re = summed[2 * side * count : (2 * side + 1) * count]
                w_im = summed[(2 * side + 1) * count : (2 * side + 2) * count]
                base = 2 * side * count * BAND + row
                shift_ref[half, pl.ds(base, count, stride=BAND), :] = t_re * w_re - t_im * w_im
                shift_ref[half, pl.ds(base + count * BAND, count, stride=BAND), :] = (
                    t_re * w_im + t_im * w_re
                )

    for side, (columns, target) in enumerate(((cols_ref, own_ref), (beside_cols_ref, out_ref))):
        for spot in range(count):
            at = columns[spot, 1]
            turn = (LANES - at) & (LANES - 1)
            for part in range(2):
                base = ((2 * side + part) * count + spot) * BAND
                left = pltpu.roll(shift_ref[0, base : base + BAND, :], turn, 1)
                right = pltpu.roll(shift_ref[1, base : base + BAND, :], turn, 1)
                target[spot, part * BAND : (part + 1) * BAND, :] = jnp.where(
                    lane < LANES - at, left, right
                )


def probe_kernel(me_ref, spots_ref, recv_ref, dft_ref, seen_ref, misfit_ref, out_ref, wave_ref, strip_ref, seen, sem):
    peers = recv_ref.shape[0]
    me = me_ref[0]
    fetch = pltpu.make_async_copy(seen_ref.at[me, 0], seen, sem)
    fetch.start()
    start_row = spots_ref[me, 0]
    start_col = spots_ref[me, 1]
    edge = MARGIN // BAND
    for part in range(2):
        for peer in range(peers):
            wave_ref[part, MARGIN + peer * BAND : MARGIN + (peer + 1) * BAND, :] = recv_ref[
                peer, part * BAND : (part + 1) * BAND, :
            ]
        for step in range(edge):
            for peer, at in ((peers - edge + step, step), (step, step + edge + peers)):
                wave_ref[part, at * BAND : (at + 1) * BAND, :] = recv_ref[
                    peer, (2 + part) * BAND : (3 + part) * BAND, :
                ]
    exit_re = wave_ref[0, pl.ds(start_row, LANES), :]
    exit_im = wave_ref[1, pl.ds(start_row, LANES), :]
    right = (dft_ref[0], dft_ref[1])
    left = (dft_ref[2], dft_ref[3])

    def transform(re, im, by_cols, by_rows):
        half = dot3(split(jnp.concatenate([re, im], 1)), by_cols)
        full = dot3(by_rows, split(jnp.concatenate([half[:, :LANES], half[:, LANES:]], 0)))
        return full[:LANES], full[LANES:]

    far_re, far_im = transform(exit_re, exit_im, right, left)
    fetch.wait()
    misfit = far_re * far_re + far_im * far_im - seen[...]
    misfit_ref[...] = misfit
    back_re, back_im = transform(misfit * far_re, misfit * far_im, left, right)
    piece = SIGMA_SCALE * (exit_re * back_im - exit_im * back_re)

    turned = pltpu.roll(piece, start_col & (LANES - 1), 1)
    lane = lax.broadcasted_iota(jnp.int32, (LANES, LANES), 1)
    strip_ref[...] = jnp.zeros(strip_ref.shape, jnp.float32)
    strip_ref[0, pl.ds(start_row, LANES), :] = jnp.where(lane >= start_col, turned, 0.0)
    strip_ref[1, pl.ds(start_row, LANES), :] = jnp.where(lane < start_col, turned, 0.0)
    for peer in range(peers):
        if peer < edge:
            beside = peer + edge + peers
        elif peer >= peers - edge:
            beside = peer - (peers - edge)
        else:
            beside = None
        for half in range(2):
            lanes = slice(half * LANES, (half + 1) * LANES)
            out_ref[peer, :BAND, lanes] = strip_ref[half, MARGIN + peer * BAND : MARGIN + (peer + 1) * BAND, :]
            out_ref[peer, BAND:, lanes] = (
                jnp.zeros((BAND, LANES), jnp.float32)
                if beside is None
                else strip_ref[half, beside * BAND : (beside + 1) * BAND, :]
            )


def beside_pairs(beams, tiles, outward):
    edge = MARGIN // BAND
    pairs = []
    for band in range(beams):
        step = -1 if band < edge else 1 if band >= beams - edge else 0
        for tile in range(tiles):
            if step and 0 <= tile + step < tiles:
                here, there = band * tiles + tile, band * tiles + tile + step
                pairs.append((here, there) if outward else (there, here))
    return pairs


def shards(
    scattering, potential, row_offset, col_offset, table_index, beam_tilt, coef_table, measured
):
    beam_dev, _, tile_rows, tile_cols = scattering.shape
    beams = lax.axis_size("beam")
    tiles = lax.axis_size("tile")
    planes = 2 * beam_dev
    count = row_offset.shape[0]
    length = measured.shape[-1]
    assert tile_rows == beams * BAND and tile_cols == 2 * LANES and length == LANES
    assert count == beams and beams * planes == LANES
    me = lax.axis_index("beam").reshape(1)

    spots = jnp.concatenate([row_offset, col_offset, table_index], 1)
    beside = lax.ppermute(spots, ("beam", "tile"), beside_pairs(beams, tiles, False))

    chunk = 2 * planes * BAND + BAND
    packed = pl.pallas_call(
        pack_kernel,
        name="pack",
        in_specs=[
            pl.BlockSpec(memory_space=SMEM),
            pl.BlockSpec(memory_space=SMEM),
            pl.BlockSpec(memory_space=SMEM),
            pl.BlockSpec(memory_space=pl.ANY),
        ],
        out_specs=pl.BlockSpec(memory_space=VMEM),
        out_shape=jax.ShapeDtypeStruct((beams, chunk, LANES), jnp.float32),
        scratch_shapes=[pltpu.SemaphoreType.DMA((2 * planes,))],
    )(me, beam_tilt, coef_table, scattering.reshape(planes, beams, BAND, tile_cols))
    bands = lax.all_to_all(packed, "beam", 0, 0, tiled=True)

    band_potential = lax.dynamic_slice_in_dim(potential, me[0] * BAND, BAND, 0)
    own, others = pl.pallas_call(
        exit_kernel,
        name="exit",
        in_specs=[pl.BlockSpec(memory_space=SMEM)] * 2 + [pl.BlockSpec(memory_space=VMEM)] * 4,
        out_specs=[pl.BlockSpec(memory_space=VMEM)] * 2,
        out_shape=[jax.ShapeDtypeStruct((count, 2 * BAND, LANES), jnp.float32)] * 2,
        scratch_shapes=[pltpu.VMEM((2, 4 * count * BAND, LANES), jnp.float32)],
    )(spots, beside, spots, beside, bands, band_potential)
    others = lax.ppermute(others, ("beam", "tile"), beside_pairs(beams, tiles, True))
    exits = lax.all_to_all(jnp.concatenate([own, others], 1), "beam", 0, 0, tiled=True)

    misfit, strips = pl.pallas_call(
        probe_kernel,
        name="probe",
        in_specs=[pl.BlockSpec(memory_space=SMEM)] * 2
        + [pl.BlockSpec(memory_space=VMEM)] * 2
        + [pl.BlockSpec(memory_space=pl.ANY)],
        out_specs=[pl.BlockSpec(memory_space=VMEM)] * 2,
        out_shape=[
            jax.ShapeDtypeStruct((length, length), jnp.float32),
            jax.ShapeDtypeStruct((beams, 2 * BAND, tile_cols), jnp.float32),
        ],
        scratch_shapes=[
            pltpu.VMEM((2, tile_rows + 2 * MARGIN, LANES), jnp.float32),
            pltpu.VMEM((2, tile_rows + 2 * MARGIN, LANES), jnp.float32),
            pltpu.VMEM((length, length), jnp.float32),
            pltpu.SemaphoreType.DMA,
        ],
    )(me, spots, exits, jnp.asarray(dft_blocks(length)), measured)

    summed = jnp.sum(lax.all_to_all(strips, "beam", 0, 0, tiled=True), 0)
    rims = lax.ppermute(summed[BAND:], ("beam", "tile"), beside_pairs(beams, tiles, False))
    band = summed[:BAND] + rims
    core = lax.all_to_all(
        jnp.broadcast_to(band[None], (beams, BAND, tile_cols)), "beam", 0, 0, tiled=True
    )
    return (misfit[None, None], core.reshape(tile_rows, tile_cols))


def solution(mesh):
    in_specs = (
        P("beam", None, "tile", None),
        P("tile", None),
        P(None, "tile"),
        P(None, "tile"),
        P(None, "tile"),
        P(None, "beam"),
        P(None, None, "beam"),
        P(None, "tile", None, None),
    )
    out_specs = (P("beam", "tile", None, None), P("tile", None))
    return jax.shard_map(shards, mesh=mesh, in_specs=in_specs, out_specs=out_specs, check_vma=False)
```

```python
import math

import jax
import jax.numpy as jnp
import numpy as np
from jax import lax
from jax.experimental import pallas as pl
from jax.experimental.pallas import tpu as pltpu
from jax.sharding import PartitionSpec as P

MARGIN = 32
SIGMA_SCALE = 1.0
LANES = 128
BAND = 8

VMEM = pltpu.MemorySpace.VMEM
SMEM = pltpu.MemorySpace.SMEM


def dft_blocks(length):
    index = np.arange(length)
    angle = (index[:, None] * index[None, :] % length) * (2.0 * math.pi / length)
    re = np.cos(angle) / math.sqrt(length)
    im = -np.sin(angle) / math.sqrt(length)
    forward = np.block([[re, im], [-im, re]]).astype(np.float32)
    parts = []
    for table in (forward, forward.T):
        high = table.astype(jnp.bfloat16)
        parts += [high, (table - high.astype(np.float32)).astype(jnp.bfloat16)]
    return np.stack(parts)


def split(value):
    high = value.astype(jnp.bfloat16)
    return high, (value - high.astype(jnp.float32)).astype(jnp.bfloat16)


def dot3(left, right):
    def dot(a, b):
        return jnp.dot(a, b, preferred_element_type=jnp.float32)

    return dot(left[0], right[0]) + (dot(left[0], right[1]) + dot(left[1], right[0]))


def pack_kernel(me_ref, tilt_ref, table_ref, waves_ref, out_ref, sem):
    planes = waves_ref.shape[0]
    copies = [
        pltpu.make_async_copy(
            waves_ref.at[plane, :, :, pl.ds(half * LANES, LANES)],
            out_ref.at[:, pl.ds((half * planes + plane) * BAND, BAND), :],
            sem.at[half * planes + plane],
        )
        for half in range(2)
        for plane in range(planes)
    ]
    for copy in copies:
        copy.start()
    sub = lax.broadcasted_iota(jnp.int32, (BAND, LANES), 0)
    lane = lax.broadcasted_iota(jnp.int32, (BAND, LANES), 1) - me_ref[0] * planes
    tile = jnp.zeros((BAND, LANES), jnp.float32)
    for beam in range(planes // 2):
        for part in range(2):
            here = lane == 2 * beam + part
            for row in range(4):
                value = table_ref[0, row, beam] if part == 0 else -table_ref[1, row, beam]
                tile = jnp.where(here & (sub == row), value, tile)
            for row in range(2):
                tile = jnp.where(here & (sub == 4 + row), tilt_ref[row, beam].astype(jnp.float32), tile)
    for peer in range(out_ref.shape[0]):
        out_ref[peer, 2 * planes * BAND :, :] = tile
    for copy in copies:
        copy.wait()


def exit_kernel(me_ref, spots_ref, beside_ref, recv_ref, potential_ref, own_ref, out_ref):
    peers = recv_ref.shape[0]
    extra = recv_ref.shape[1] - BAND
    planes = extra // (2 * BAND)
    count = spots_ref.shape[0]

    table = recv_ref[0, extra:, :]
    for peer in range(1, peers):
        table = table + recv_ref[peer, extra:, :]
    lane = lax.broadcasted_iota(jnp.int32, (BAND, LANES), 1)
    swapped = jnp.where(
        lane % 2 == 0, -pltpu.roll(table, LANES - 1, 1), pltpu.roll(table, 1, 1)
    )
    tilt_row = table[4:5].astype(jnp.int32)
    tilt_col = table[5:6].astype(jnp.int32)

    def coefs(ref):
        row = ref[:, 0:1] - MARGIN
        col = ref[:, 1:2]
        pick = ref[:, 2:3]
        turns = (tilt_row * row + tilt_col * col) & (LANES - 1)
        angle = turns.astype(jnp.float32) * (2.0 * math.pi / LANES)
        u = jnp.zeros((count, LANES), jnp.float32)
        v = jnp.zeros((count, LANES), jnp.float32)
        for n in range(4):
            u = jnp.where(pick == n, table[n : n + 1], u)
            v = jnp.where(pick == n, swapped[n : n + 1], v)
        cosine = jnp.cos(angle)
        sine = jnp.sin(angle)
        return u * cosine + v * sine, v * cosine - u * sine

    weights = split(jnp.concatenate(coefs(spots_ref) + coefs(beside_ref), 0))
    local = potential_ref[...] * SIGMA_SCALE
    trans_re = jnp.cos(local)
    trans_im = jnp.sin(local)
    wide = lax.broadcasted_iota(jnp.int32, (count, LANES), 1)

    for row in range(BAND):
        waves = jnp.concatenate(
            [
                jnp.concatenate(
                    [
                        recv_ref[peer, pl.ds(half * planes * BAND + row, planes, stride=BAND), :]
                        for peer in range(peers)
                    ],
                    0,
                )
                for half in range(2)
            ],
            1,
        )
        summed = dot3(weights, split(waves))
        slot = me_ref[0] * BAND + row
        for side, (ref, target) in enumerate(((spots_ref, own_ref), (beside_ref, out_ref))):
            left = wide >= ref[:, 1:2]
            start = ref[:, 0:1] - MARGIN
            inside = (start <= slot) & (start + LANES > slot)
            keep = inside if side == 0 else ~inside

            def cut(value):
                return jnp.where(left, value[:, :LANES], value[:, LANES:])

            w_re = cut(summed[2 * side * count : (2 * side + 1) * count])
            w_im = cut(summed[(2 * side + 1) * count : (2 * side + 2) * count])
            t_re = cut(trans_re[row : row + 1])
            t_im = cut(trans_im[row : row + 1])
            for part, value in enumerate((t_re * w_re - t_im * w_im, t_re * w_im + t_im * w_re)):
                target[pl.ds(part * BAND + row, count, stride=2 * BAND), :] = jnp.where(
                    keep, value, 0.0
                )


def probe_kernel(me_ref, recv_ref, dft_ref, seen_ref, misfit_ref, out_ref, seen, sem):
    fetch = pltpu.make_async_copy(seen_ref.at[me_ref[0], 0], seen, sem)
    fetch.start()
    exit_re = recv_ref[:, :BAND, :].reshape(LANES, LANES)
    exit_im = recv_ref[:, BAND:, :].reshape(LANES, LANES)
    right = (dft_ref[0], dft_ref[1])
    left = (dft_ref[2], dft_ref[3])

    def transform(re, im, by_cols, by_rows):
        half = dot3(split(jnp.concatenate([re, im], 1)), by_cols)
        full = dot3(by_rows, split(jnp.concatenate([half[:, :LANES], half[:, LANES:]], 0)))
        return full[:LANES], full[LANES:]

    far_re, far_im = transform(exit_re, exit_im, right, left)
    fetch.wait()
    misfit = far_re * far_re + far_im * far_im - seen[...]
    misfit_ref[...] = misfit
    back_re, back_im = transform(misfit * far_re, misfit * far_im, left, right)
    out_ref[...] = (SIGMA_SCALE * (exit_re * back_im - exit_im * back_re)).reshape(out_ref.shape)


def place_kernel(me_ref, spots_ref, recv_ref, core_ref, rim_ref):
    slot = lax.broadcasted_iota(jnp.int32, (BAND, LANES), 0) + me_ref[0] * BAND
    lane = lax.broadcasted_iota(jnp.int32, (BAND, LANES), 1)
    sums = [jnp.zeros((BAND, LANES), jnp.float32)] * 4
    for spot in range(recv_ref.shape[0]):
        start = spots_ref[spot, 0] - MARGIN
        inside = (slot >= start) & (slot < start + LANES)
        left = lane >= spots_ref[spot, 1]
        piece = recv_ref[spot]
        core = jnp.where(inside, piece, 0.0)
        rim = jnp.where(inside, 0.0, piece)
        parts = (jnp.where(left, core, 0.0), jnp.where(left, 0.0, core), jnp.where(left, rim, 0.0), jnp.where(left, 0.0, rim))
        sums = [total + part for total, part in zip(sums, parts)]
    core_ref[:, :LANES], core_ref[:, LANES:], rim_ref[:, :LANES], rim_ref[:, LANES:] = sums


def on_chip(shape):
    return pltpu.VMEM(shape, jnp.float32)


def near(value):
    return pltpu.with_memory_space_constraint(value, VMEM)


def beside_pairs(beams, tiles, outward):
    edge = MARGIN // BAND
    pairs = []
    for band in range(beams):
        step = -1 if band < edge else 1 if band >= beams - edge else 0
        for tile in range(tiles):
            if step and 0 <= tile + step < tiles:
                here, there = band * tiles + tile, band * tiles + tile + step
                pairs.append((here, there) if outward else (there, here))
    return pairs


def shards(
    scattering, potential, row_offset, col_offset, table_index, beam_tilt, coef_table, measured
):
    beam_dev, _, tile_rows, tile_cols = scattering.shape
    beams = lax.axis_size("beam")
    tiles = lax.axis_size("tile")
    planes = 2 * beam_dev
    count = row_offset.shape[0]
    length = measured.shape[-1]
    assert tile_rows == beams * BAND and tile_cols == 2 * LANES and length == LANES
    assert count == beams and beams * planes == LANES
    me = lax.axis_index("beam").reshape(1)
    smem = pl.BlockSpec(memory_space=SMEM)
    vmem = pl.BlockSpec(memory_space=VMEM)
    anywhere = pl.BlockSpec(memory_space=pl.ANY)

    spots = jnp.concatenate([row_offset, col_offset, table_index], 1)
    beside = lax.ppermute(spots, ("beam", "tile"), beside_pairs(beams, tiles, False))

    chunk = 2 * planes * BAND + BAND
    packed = pl.pallas_call(
        pack_kernel,
        name="pack",
        in_specs=[smem, smem, smem, anywhere],
        out_specs=vmem,
        out_shape=on_chip((beams, chunk, LANES)),
        scratch_shapes=[pltpu.SemaphoreType.DMA((2 * planes,))],
    )(me, beam_tilt, coef_table, scattering.reshape(planes, beams, BAND, tile_cols))
    bands = lax.all_to_all(packed, "beam", 0, 0, tiled=True)

    band_potential = lax.dynamic_slice_in_dim(potential, me[0] * BAND, BAND, 0)
    own, others = pl.pallas_call(
        exit_kernel,
        name="exit",
        in_specs=[smem] + [vmem] * 4,
        out_specs=[vmem] * 2,
        out_shape=[on_chip((count * 2 * BAND, LANES))] * 2,
    )(me, spots, beside, near(bands), band_potential)
    others = lax.ppermute(others, ("beam", "tile"), beside_pairs(beams, tiles, True))
    exits = lax.all_to_all((own + others).reshape(count, 2 * BAND, LANES), "beam", 0, 0, tiled=True)

    misfit, pieces = pl.pallas_call(
        probe_kernel,
        name="probe",
        in_specs=[smem, vmem, vmem, anywhere],
        out_specs=[vmem] * 2,
        out_shape=[
            jax.ShapeDtypeStruct((length, length), jnp.float32),
            on_chip((beams, BAND, LANES)),
        ],
        scratch_shapes=[pltpu.VMEM((length, length), jnp.float32), pltpu.SemaphoreType.DMA],
    )(me, near(exits), jnp.asarray(dft_blocks(length)), measured)
    pieces = lax.all_to_all(pieces, "beam", 0, 0, tiled=True)

    band, rims = pl.pallas_call(
        place_kernel,
        name="place",
        in_specs=[smem, smem, vmem],
        out_specs=[vmem] * 2,
        out_shape=[on_chip((BAND, tile_cols))] * 2,
    )(me, spots, near(pieces))
    band = band + lax.ppermute(rims, ("beam", "tile"), beside_pairs(beams, tiles, False))
    core = lax.all_to_all(
        jnp.broadcast_to(band[None], (beams, BAND, tile_cols)), "beam", 0, 0, tiled=True
    )
    return (misfit[None, None], core.reshape(tile_rows, tile_cols))


def solution(mesh):
    in_specs = (
        P("beam", None, "tile", None),
        P("tile", None),
        P(None, "tile"),
        P(None, "tile"),
        P(None, "tile"),
        P(None, "beam"),
        P(None, None, "beam"),
        P(None, "tile", None, None),
    )
    out_specs = (P("beam", "tile", None, None), P("tile", None))
    return jax.shard_map(shards, mesh=mesh, in_specs=in_specs, out_specs=out_specs, check_vma=False)
```

```python
import math

import jax
import jax.numpy as jnp
import numpy as np
from jax import lax
from jax.experimental import pallas as pl
from jax.experimental.pallas import tpu as pltpu
from jax.sharding import PartitionSpec as P

MARGIN = 32
SIGMA_SCALE = 1.0
LANES = 128
BAND = 8
SPAN = 2

VMEM = pltpu.MemorySpace.VMEM
SMEM = pltpu.MemorySpace.SMEM


def dft_blocks(length):
    index = np.arange(length)
    angle = (index[:, None] * index[None, :] % length) * (2.0 * math.pi / length)
    re = np.cos(angle) / math.sqrt(length)
    im = -np.sin(angle) / math.sqrt(length)
    forward = np.block([[re, im], [-im, re]]).astype(np.float32)
    parts = []
    for table in (forward, forward.T):
        high = table.astype(jnp.bfloat16)
        parts += [high, (table - high.astype(np.float32)).astype(jnp.bfloat16)]
    return np.stack(parts)


def split(value):
    high = value.astype(jnp.bfloat16)
    return high, (value - high.astype(jnp.float32)).astype(jnp.bfloat16)


def dot3(left, right):
    def dot(a, b):
        return jnp.dot(a, b, preferred_element_type=jnp.float32)

    return dot(left[0], right[0]) + (dot(left[0], right[1]) + dot(left[1], right[0]))


def pack_kernel(me_ref, tilt_ref, table_ref, waves_ref, out_ref, held, extra, in_sem, out_sem, extra_sem):
    planes = waves_ref.shape[0]
    loads = [
        pltpu.make_async_copy(waves_ref.at[plane], held.at[plane], in_sem.at[plane])
        for plane in range(planes)
    ]
    for load in loads:
        load.start()
    sub = lax.broadcasted_iota(jnp.int32, (BAND, LANES), 0)
    lane = lax.broadcasted_iota(jnp.int32, (BAND, LANES), 1) - me_ref[0] * planes
    tile = jnp.zeros((BAND, LANES), jnp.float32)
    for beam in range(planes // 2):
        for part in range(2):
            here = lane == 2 * beam + part
            for row in range(4):
                value = table_ref[0, row, beam] if part == 0 else -table_ref[1, row, beam]
                tile = jnp.where(here & (sub == row), value, tile)
            for row in range(2):
                tile = jnp.where(here & (sub == 4 + row), tilt_ref[row, beam].astype(jnp.float32), tile)
    for peer in range(out_ref.shape[0]):
        extra[peer] = tile
    stores = [
        pltpu.make_async_copy(extra, out_ref.at[:, pl.ds(2 * planes * BAND, BAND), :], extra_sem)
    ]
    stores[0].start()
    for plane in range(planes):
        loads[plane].wait()
        for half in range(2):
            store = pltpu.make_async_copy(
                held.at[plane, :, :, pl.ds(half * LANES, LANES)],
                out_ref.at[:, pl.ds((half * planes + plane) * BAND, BAND), :],
                out_sem.at[half * planes + plane],
            )
            store.start()
            stores.append(store)
    for store in stores:
        store.wait()


def exit_kernel(me_ref, spots_ref, beside_ref, recv_ref, potential_ref, own_ref, out_ref):
    peers = recv_ref.shape[0]
    extra = recv_ref.shape[1] - BAND
    planes = extra // (2 * BAND)
    count = spots_ref.shape[0]

    table = recv_ref[0, extra:, :]
    for peer in range(1, peers):
        table = table + recv_ref[peer, extra:, :]
    lane = lax.broadcasted_iota(jnp.int32, (BAND, LANES), 1)
    swapped = jnp.where(
        lane % 2 == 0, -pltpu.roll(table, LANES - 1, 1), pltpu.roll(table, 1, 1)
    )
    tilt_row = table[4:5].astype(jnp.int32)
    tilt_col = table[5:6].astype(jnp.int32)

    def coefs(ref):
        row = ref[:, 0:1] - MARGIN
        col = ref[:, 1:2]
        pick = ref[:, 2:3]
        turns = (tilt_row * row + tilt_col * col) & (LANES - 1)
        angle = turns.astype(jnp.float32) * (2.0 * math.pi / LANES)
        u = jnp.zeros((count, LANES), jnp.float32)
        v = jnp.zeros((count, LANES), jnp.float32)
        for n in range(4):
            u = jnp.where(pick == n, table[n : n + 1], u)
            v = jnp.where(pick == n, swapped[n : n + 1], v)
        cosine = jnp.cos(angle)
        sine = jnp.sin(angle)
        return u * cosine + v * sine, v * cosine - u * sine

    weights = split(jnp.concatenate(coefs(spots_ref) + coefs(beside_ref), 0))
    local = potential_ref[...] * SIGMA_SCALE
    trans_re = jnp.cos(local)
    trans_im = jnp.sin(local)
    wide = lax.broadcasted_iota(jnp.int32, (count, LANES), 1)

    for row in range(BAND):
        waves = jnp.concatenate(
            [
                jnp.concatenate(
                    [
                        recv_ref[peer, pl.ds(half * planes * BAND + row, planes, stride=BAND), :]
                        for peer in range(peers)
                    ],
                    0,
                )
                for half in range(2)
            ],
            1,
        )
        summed = dot3(weights, split(waves))
        slot = me_ref[0] * BAND + row
        for side, (ref, target) in enumerate(((spots_ref, own_ref), (beside_ref, out_ref))):
            left = wide >= ref[:, 1:2]
            start = ref[:, 0:1] - MARGIN
            inside = (start <= slot) & (start + LANES > slot)
            keep = inside if side == 0 else ~inside

            def cut(value):
                return jnp.where(left, value[:, :LANES], value[:, LANES:])

            w_re = cut(summed[2 * side * count : (2 * side + 1) * count])
            w_im = cut(summed[(2 * side + 1) * count : (2 * side + 2) * count])
            t_re = cut(trans_re[row : row + 1])
            t_im = cut(trans_im[row : row + 1])
            for part, value in enumerate((t_re * w_re - t_im * w_im, t_re * w_im + t_im * w_re)):
                target[pl.ds(part * BAND + row, count, stride=2 * BAND), :] = jnp.where(
                    keep, value, 0.0
                )


def probe_kernel(me_ref, recv_ref, dft_ref, seen_ref, misfit_ref, out_ref, seen, sem):
    fetch = pltpu.make_async_copy(seen_ref.at[me_ref[0], 0], seen, sem)
    fetch.start()
    exit_re = recv_ref[:, :BAND, :].reshape(LANES, LANES)
    exit_im = recv_ref[:, BAND:, :].reshape(LANES, LANES)
    right = (dft_ref[0], dft_ref[1])
    left = (dft_ref[2], dft_ref[3])

    def transform(re, im, by_cols, by_rows):
        half = dot3(split(jnp.concatenate([re, im], 1)), by_cols)
        full = dot3(by_rows, split(jnp.concatenate([half[:, :LANES], half[:, LANES:]], 0)))
        return full[:LANES], full[LANES:]

    far_re, far_im = transform(exit_re, exit_im, right, left)
    fetch.wait()
    misfit = far_re * far_re + far_im * far_im - seen[...]
    misfit_ref[...] = misfit
    back_re, back_im = transform(misfit * far_re, misfit * far_im, left, right)
    piece = SIGMA_SCALE * (exit_re * back_im - exit_im * back_re)
    peers, rows, _ = out_ref.shape
    for peer in range(peers):
        at = peer // SPAN * rows
        out_ref[peer] = piece[at : at + rows]


def place_kernel(me_ref, spots_ref, recv_ref, core_ref, rim_ref):
    shape = recv_ref.shape[1:]
    slot = lax.broadcasted_iota(jnp.int32, shape, 0) + me_ref[0] // SPAN * shape[0]
    lane = lax.broadcasted_iota(jnp.int32, shape, 1)
    sums = [jnp.zeros(shape, jnp.float32)] * 4
    for spot in range(recv_ref.shape[0]):
        start = spots_ref[spot, 0] - MARGIN
        inside = (slot >= start) & (slot < start + LANES)
        left = lane >= spots_ref[spot, 1]
        piece = recv_ref[spot]
        core = jnp.where(inside, piece, 0.0)
        rim = jnp.where(inside, 0.0, piece)
        parts = (jnp.where(left, core, 0.0), jnp.where(left, 0.0, core), jnp.where(left, rim, 0.0), jnp.where(left, 0.0, rim))
        sums = [total + part for total, part in zip(sums, parts)]
    core_ref[:, :LANES], core_ref[:, LANES:], rim_ref[:, :LANES], rim_ref[:, LANES:] = sums


def on_chip(shape):
    return pltpu.VMEM(shape, jnp.float32)


def near(value):
    return pltpu.with_memory_space_constraint(value, VMEM)


def beside_pairs(beams, tiles, outward):
    edge = MARGIN // BAND
    pairs = []
    for band in range(beams):
        step = -1 if band < edge else 1 if band >= beams - edge else 0
        for tile in range(tiles):
            if step and 0 <= tile + step < tiles:
                here, there = band * tiles + tile, band * tiles + tile + step
                pairs.append((here, there) if outward else (there, here))
    return pairs


def shards(
    scattering, potential, row_offset, col_offset, table_index, beam_tilt, coef_table, measured
):
    beam_dev, _, tile_rows, tile_cols = scattering.shape
    beams = lax.axis_size("beam")
    tiles = lax.axis_size("tile")
    planes = 2 * beam_dev
    count = row_offset.shape[0]
    length = measured.shape[-1]
    assert tile_rows == beams * BAND and tile_cols == 2 * LANES and length == LANES
    assert count == beams and beams * planes == LANES
    me = lax.axis_index("beam").reshape(1)
    smem = pl.BlockSpec(memory_space=SMEM)
    vmem = pl.BlockSpec(memory_space=VMEM)
    anywhere = pl.BlockSpec(memory_space=pl.ANY)

    spots = jnp.concatenate([row_offset, col_offset, table_index], 1)
    beside = lax.ppermute(spots, ("beam", "tile"), beside_pairs(beams, tiles, False))

    chunk = 2 * planes * BAND + BAND
    packed = pl.pallas_call(
        pack_kernel,
        name="pack",
        in_specs=[smem, smem, smem, anywhere],
        out_specs=anywhere,
        out_shape=jax.ShapeDtypeStruct((beams, chunk, LANES), jnp.float32),
        scratch_shapes=[
            pltpu.VMEM((planes, beams, BAND, tile_cols), jnp.float32),
            pltpu.VMEM((beams, BAND, LANES), jnp.float32),
            pltpu.SemaphoreType.DMA((planes,)),
            pltpu.SemaphoreType.DMA((2 * planes,)),
            pltpu.SemaphoreType.DMA,
        ],
    )(me, beam_tilt, coef_table, scattering.reshape(planes, beams, BAND, tile_cols))
    bands = lax.all_to_all(packed, "beam", 0, 0, tiled=True)

    band_potential = lax.dynamic_slice_in_dim(potential, me[0] * BAND, BAND, 0)
    own, others = pl.pallas_call(
        exit_kernel,
        name="exit",
        in_specs=[smem] + [vmem] * 4,
        out_specs=[vmem] * 2,
        out_shape=[on_chip((count * 2 * BAND, LANES))] * 2,
    )(me, spots, beside, near(bands), band_potential)
    others = lax.ppermute(others, ("beam", "tile"), beside_pairs(beams, tiles, True))
    exits = lax.all_to_all((own + others).reshape(count, 2 * BAND, LANES), "beam", 0, 0, tiled=True)

    misfit, pieces = pl.pallas_call(
        probe_kernel,
        name="probe",
        in_specs=[smem, vmem, vmem, anywhere],
        out_specs=[vmem] * 2,
        out_shape=[
            jax.ShapeDtypeStruct((length, length), jnp.float32),
            on_chip((beams, SPAN * BAND, LANES)),
        ],
        scratch_shapes=[pltpu.VMEM((length, length), jnp.float32), pltpu.SemaphoreType.DMA],
    )(me, near(exits), near(jnp.asarray(dft_blocks(length))), measured)
    pieces = lax.all_to_all(pieces, "beam", 0, 0, tiled=True)

    band, rims = pl.pallas_call(
        place_kernel,
        name="place",
        in_specs=[smem, smem, vmem],
        out_specs=[vmem] * 2,
        out_shape=[on_chip((SPAN * BAND, tile_cols))] * 2,
    )(me, spots, near(pieces))
    band = band + lax.ppermute(rims, ("beam", "tile"), beside_pairs(beams, tiles, False))
    groups = [list(range(at, beams, SPAN)) for at in range(SPAN)]
    core = lax.all_to_all(
        jnp.broadcast_to(band[None], (beams // SPAN, SPAN * BAND, tile_cols)),
        "beam",
        0,
        0,
        axis_index_groups=groups,
        tiled=True,
    )
    return (misfit[None, None], core.reshape(tile_rows, tile_cols))


def solution(mesh):
    in_specs = (
        P("beam", None, "tile", None),
        P("tile", None),
        P(None, "tile"),
        P(None, "tile"),
        P(None, "tile"),
        P(None, "beam"),
        P(None, None, "beam"),
        P(None, "tile", None, None),
    )
    out_specs = (P("beam", "tile", None, None), P("tile", None))
    return jax.shard_map(shards, mesh=mesh, in_specs=in_specs, out_specs=out_specs, check_vma=False)
```

```python
import math

import jax
import jax.numpy as jnp
import numpy as np
from jax import lax
from jax.experimental import pallas as pl
from jax.experimental.pallas import tpu as pltpu
from jax.sharding import PartitionSpec as P

MARGIN = 32
SIGMA_SCALE = 1.0
LANES = 128
BAND = 8
SPAN = 2

VMEM = pltpu.MemorySpace.VMEM


def dft_blocks(length):
    index = np.arange(length)
    angle = (index[:, None] * index[None, :] % length) * (2.0 * math.pi / length)
    re = np.cos(angle) / math.sqrt(length)
    im = -np.sin(angle) / math.sqrt(length)
    forward = np.block([[re, im], [-im, re]]).astype(np.float32)
    parts = []
    for table in (forward, forward.T):
        high = table.astype(jnp.bfloat16)
        parts += [high, (table - high.astype(np.float32)).astype(jnp.bfloat16)]
    return np.stack(parts)


def split(value):
    high = value.astype(jnp.bfloat16)
    return high, (value - high.astype(jnp.float32)).astype(jnp.bfloat16)


def dot3(left, right):
    def dot(a, b):
        return jnp.dot(a, b, preferred_element_type=jnp.float32)

    return dot(left[0], right[0]) + (dot(left[0], right[1]) + dot(left[1], right[0]))


def pack_kernel(
    tilt_hbm,
    table_hbm,
    waves_ref,
    potential_ref,
    measured_ref,
    out_ref,
    band_ref,
    seen_ref,
    held,
    extra,
    tilt_ref,
    table_ref,
    in_sem,
    out_sem,
    small_sem,
):
    planes = waves_ref.shape[0]
    me = lax.axis_index("beam")
    later = [
        pltpu.make_async_copy(potential_ref.at[pl.ds(me * BAND, BAND)], band_ref, small_sem.at[3]),
        pltpu.make_async_copy(measured_ref.at[me, 0], seen_ref, small_sem.at[4]),
    ]
    small = [
        pltpu.make_async_copy(tilt_hbm, tilt_ref, small_sem.at[0]),
        pltpu.make_async_copy(table_hbm, table_ref, small_sem.at[1]),
    ]
    loads = [
        pltpu.make_async_copy(waves_ref.at[plane], held.at[plane], in_sem.at[plane])
        for plane in range(planes)
    ]
    for load in small + loads + later:
        load.start()
    for load in small:
        load.wait()
    sub = lax.broadcasted_iota(jnp.int32, (BAND, LANES), 0)
    lane = lax.broadcasted_iota(jnp.int32, (BAND, LANES), 1) - me * planes
    tile = jnp.zeros((BAND, LANES), jnp.float32)
    for beam in range(planes // 2):
        for part in range(2):
            here = lane == 2 * beam + part
            for row in range(4):
                value = table_ref[0, row, beam] if part == 0 else -table_ref[1, row, beam]
                tile = jnp.where(here & (sub == row), value, tile)
            for row in range(2):
                tile = jnp.where(here & (sub == 4 + row), tilt_ref[row, beam].astype(jnp.float32), tile)
    for peer in range(out_ref.shape[0]):
        extra[peer] = tile
    stores = [
        pltpu.make_async_copy(extra, out_ref.at[:, pl.ds(2 * planes * BAND, BAND), :], small_sem.at[2])
    ]
    stores[0].start()
    for plane in range(planes):
        loads[plane].wait()
        for half in range(2):
            store = pltpu.make_async_copy(
                held.at[plane, :, :, pl.ds(half * LANES, LANES)],
                out_ref.at[:, pl.ds((half * planes + plane) * BAND, BAND), :],
                out_sem.at[half * planes + plane],
            )
            store.start()
            stores.append(store)
    for copy in stores + later:
        copy.wait()


def exit_kernel(spots_ref, beside_ref, recv_ref, potential_ref, own_ref, out_ref):
    peers = recv_ref.shape[0]
    extra = recv_ref.shape[1] - BAND
    planes = extra // (2 * BAND)
    count = spots_ref.shape[0]

    table = recv_ref[0, extra:, :]
    for peer in range(1, peers):
        table = table + recv_ref[peer, extra:, :]
    lane = lax.broadcasted_iota(jnp.int32, (BAND, LANES), 1)
    swapped = jnp.where(
        lane % 2 == 0, -pltpu.roll(table, LANES - 1, 1), pltpu.roll(table, 1, 1)
    )
    tilt_row = table[4:5].astype(jnp.int32)
    tilt_col = table[5:6].astype(jnp.int32)

    def coefs(ref):
        row = ref[:, 0:1] - MARGIN
        col = ref[:, 1:2]
        pick = ref[:, 2:3]
        turns = (tilt_row * row + tilt_col * col) & (LANES - 1)
        angle = turns.astype(jnp.float32) * (2.0 * math.pi / LANES)
        u = jnp.zeros((count, LANES), jnp.float32)
        v = jnp.zeros((count, LANES), jnp.float32)
        for n in range(4):
            u = jnp.where(pick == n, table[n : n + 1], u)
            v = jnp.where(pick == n, swapped[n : n + 1], v)
        cosine = jnp.cos(angle)
        sine = jnp.sin(angle)
        return u * cosine + v * sine, v * cosine - u * sine

    weights = split(jnp.concatenate(coefs(spots_ref) + coefs(beside_ref), 0))
    local = potential_ref[...] * SIGMA_SCALE
    trans_re = jnp.cos(local)
    trans_im = jnp.sin(local)
    wide = lax.broadcasted_iota(jnp.int32, (count, LANES), 1)

    for row in range(BAND):
        waves = jnp.concatenate(
            [
                jnp.concatenate(
                    [
                        recv_ref[peer, pl.ds(half * planes * BAND + row, planes, stride=BAND), :]
                        for peer in range(peers)
                    ],
                    0,
                )
                for half in range(2)
            ],
            1,
        )
        summed = dot3(weights, split(waves))
        slot = lax.axis_index("beam") * BAND + row
        for side, (ref, target) in enumerate(((spots_ref, own_ref), (beside_ref, out_ref))):
            left = wide >= ref[:, 1:2]
            start = ref[:, 0:1] - MARGIN
            inside = (start <= slot) & (start + LANES > slot)
            keep = inside if side == 0 else ~inside

            def cut(value):
                return jnp.where(left, value[:, :LANES], value[:, LANES:])

            w_re = cut(summed[2 * side * count : (2 * side + 1) * count])
            w_im = cut(summed[(2 * side + 1) * count : (2 * side + 2) * count])
            t_re = cut(trans_re[row : row + 1])
            t_im = cut(trans_im[row : row + 1])
            for part, value in enumerate((t_re * w_re - t_im * w_im, t_re * w_im + t_im * w_re)):
                target[pl.ds(part * BAND + row, count, stride=2 * BAND), :] = jnp.where(
                    keep, value, 0.0
                )


def probe_kernel(recv_ref, dft_ref, seen_ref, misfit_ref, out_ref):
    exit_re = recv_ref[:, :BAND, :].reshape(LANES, LANES)
    exit_im = recv_ref[:, BAND:, :].reshape(LANES, LANES)
    right = (dft_ref[0], dft_ref[1])
    left = (dft_ref[2], dft_ref[3])

    def transform(re, im, by_cols, by_rows):
        half = dot3(split(jnp.concatenate([re, im], 1)), by_cols)
        full = dot3(by_rows, split(jnp.concatenate([half[:, :LANES], half[:, LANES:]], 0)))
        return full[:LANES], full[LANES:]

    far_re, far_im = transform(exit_re, exit_im, right, left)
    misfit = far_re * far_re + far_im * far_im - seen_ref[...]
    misfit_ref[...] = misfit
    back_re, back_im = transform(misfit * far_re, misfit * far_im, left, right)
    piece = SIGMA_SCALE * (exit_re * back_im - exit_im * back_re)
    peers, rows, _ = out_ref.shape
    for peer in range(peers):
        at = peer // SPAN * rows
        out_ref[peer] = piece[at : at + rows]


def place_kernel(spots_ref, recv_ref, core_ref, rim_ref):
    shape = recv_ref.shape[1:]
    slot = lax.broadcasted_iota(jnp.int32, shape, 0) + lax.axis_index("beam") // SPAN * shape[0]
    lane = lax.broadcasted_iota(jnp.int32, shape, 1)
    sums = [jnp.zeros(shape, jnp.float32)] * 4
    for spot in range(recv_ref.shape[0]):
        start = spots_ref[spot : spot + 1, 0:1] - MARGIN
        inside = (slot >= start) & (slot < start + LANES)
        left = lane >= spots_ref[spot : spot + 1, 1:2]
        piece = recv_ref[spot]
        core = jnp.where(inside, piece, 0.0)
        rim = jnp.where(inside, 0.0, piece)
        parts = (jnp.where(left, core, 0.0), jnp.where(left, 0.0, core), jnp.where(left, rim, 0.0), jnp.where(left, 0.0, rim))
        sums = [total + part for total, part in zip(sums, parts)]
    core_ref[:, :LANES], core_ref[:, LANES:], rim_ref[:, :LANES], rim_ref[:, LANES:] = sums


def on_chip(shape):
    return pltpu.VMEM(shape, jnp.float32)


def near(value):
    return pltpu.with_memory_space_constraint(value, VMEM)


def beside_pairs(beams, tiles, outward):
    edge = MARGIN // BAND
    pairs = []
    for band in range(beams):
        step = -1 if band < edge else 1 if band >= beams - edge else 0
        for tile in range(tiles):
            if step and 0 <= tile + step < tiles:
                here, there = band * tiles + tile, band * tiles + tile + step
                pairs.append((here, there) if outward else (there, here))
    return pairs


def shards(
    scattering, potential, row_offset, col_offset, table_index, beam_tilt, coef_table, measured
):
    beam_dev, _, tile_rows, tile_cols = scattering.shape
    beams = lax.axis_size("beam")
    tiles = lax.axis_size("tile")
    planes = 2 * beam_dev
    count = row_offset.shape[0]
    length = measured.shape[-1]
    assert tile_rows == beams * BAND and tile_cols == 2 * LANES and length == LANES
    assert count == beams and beams * planes == LANES
    vmem = pl.BlockSpec(memory_space=VMEM)
    anywhere = pl.BlockSpec(memory_space=pl.ANY)

    spots = jnp.concatenate([row_offset, col_offset, table_index], 1)
    beside = near(lax.ppermute(spots, ("beam", "tile"), beside_pairs(beams, tiles, False)))
    spots = near(spots)

    chunk = 2 * planes * BAND + BAND
    packed, band_potential, seen = pl.pallas_call(
        pack_kernel,
        name="pack",
        in_specs=[anywhere] * 5,
        out_specs=[anywhere, vmem, vmem],
        out_shape=[
            jax.ShapeDtypeStruct((beams, chunk, LANES), jnp.float32),
            on_chip((BAND, tile_cols)),
            on_chip((length, length)),
        ],
        scratch_shapes=[
            pltpu.VMEM((planes, beams, BAND, tile_cols), jnp.float32),
            pltpu.VMEM((beams, BAND, LANES), jnp.float32),
            pltpu.SMEM(beam_tilt.shape, beam_tilt.dtype),
            pltpu.SMEM(coef_table.shape, coef_table.dtype),
            pltpu.SemaphoreType.DMA((planes,)),
            pltpu.SemaphoreType.DMA((2 * planes,)),
            pltpu.SemaphoreType.DMA((5,)),
        ],
    )(beam_tilt, coef_table, scattering.reshape(planes, beams, BAND, tile_cols), potential, measured)
    bands = lax.all_to_all(packed, "beam", 0, 0, tiled=True)

    own, others = pl.pallas_call(
        exit_kernel,
        name="exit",
        in_specs=[vmem] * 4,
        out_specs=[vmem] * 2,
        out_shape=[on_chip((count * 2 * BAND, LANES))] * 2,
    )(spots, beside, near(bands), near(band_potential))
    others = lax.ppermute(others, ("beam", "tile"), beside_pairs(beams, tiles, True))
    exits = lax.all_to_all((own + others).reshape(count, 2 * BAND, LANES), "beam", 0, 0, tiled=True)

    misfit, pieces = pl.pallas_call(
        probe_kernel,
        name="probe",
        in_specs=[vmem] * 3,
        out_specs=[vmem] * 2,
        out_shape=[
            jax.ShapeDtypeStruct((length, length), jnp.float32),
            on_chip((beams, SPAN * BAND, LANES)),
        ],
    )(near(exits), near(jnp.asarray(dft_blocks(length))), near(seen))
    pieces = lax.all_to_all(pieces, "beam", 0, 0, tiled=True)

    band, rims = pl.pallas_call(
        place_kernel,
        name="place",
        in_specs=[vmem] * 2,
        out_specs=[vmem] * 2,
        out_shape=[on_chip((SPAN * BAND, tile_cols))] * 2,
    )(spots, near(pieces))
    band = band + lax.ppermute(rims, ("beam", "tile"), beside_pairs(beams, tiles, False))
    groups = [list(range(at, beams, SPAN)) for at in range(SPAN)]
    core = lax.all_to_all(
        jnp.broadcast_to(band[None], (beams // SPAN, SPAN * BAND, tile_cols)),
        "beam",
        0,
        0,
        axis_index_groups=groups,
        tiled=True,
    )
    return (misfit[None, None], core.reshape(tile_rows, tile_cols))


def solution(mesh):
    in_specs = (
        P("beam", None, "tile", None),
        P("tile", None),
        P(None, "tile"),
        P(None, "tile"),
        P(None, "tile"),
        P(None, "beam"),
        P(None, None, "beam"),
        P(None, "tile", None, None),
    )
    out_specs = (P("beam", "tile", None, None), P("tile", None))
    return jax.shard_map(shards, mesh=mesh, in_specs=in_specs, out_specs=out_specs, check_vma=False)
```

```python
import math

import jax
import jax.numpy as jnp
import numpy as np
from jax import lax
from jax.experimental import pallas as pl
from jax.experimental.pallas import tpu as pltpu
from jax.sharding import PartitionSpec as P

MARGIN = 32
SIGMA_SCALE = 1.0
LANES = 128
BAND = 8
SPAN = 2
PARTS = 3

VMEM = pltpu.MemorySpace.VMEM


def dft_blocks(length):
    index = np.arange(length)
    angle = (index[:, None] * index[None, :] % length) * (2.0 * math.pi / length)
    re = np.cos(angle) / math.sqrt(length)
    im = -np.sin(angle) / math.sqrt(length)
    forward = np.block([[re, im], [-im, re]]).astype(np.float32)
    parts = []
    for table in (forward, forward.T):
        rest = table
        for _ in range(PARTS):
            part = rest.astype(jnp.bfloat16)
            rest = rest - part.astype(np.float32)
            parts.append(part)
    return np.stack(parts)


def split(value):
    parts = []
    for _ in range(PARTS):
        part = value.astype(jnp.bfloat16)
        value = value - part.astype(jnp.float32)
        parts.append(part)
    return parts


def exact_dot(left, right):
    total = None
    for order in reversed(range(PARTS)):
        for at in range(order + 1):
            product = jnp.dot(left[at], right[order - at], preferred_element_type=jnp.float32)
            total = product if total is None else total + product
    return total


def pack_kernel(
    tilt_hbm,
    table_hbm,
    waves_ref,
    potential_ref,
    measured_ref,
    out_ref,
    band_ref,
    seen_ref,
    held,
    extra,
    tilt_ref,
    table_ref,
    in_sem,
    out_sem,
    small_sem,
):
    planes = waves_ref.shape[0]
    me = lax.axis_index("beam")
    later = [
        pltpu.make_async_copy(potential_ref.at[pl.ds(me * BAND, BAND)], band_ref, small_sem.at[3]),
        pltpu.make_async_copy(measured_ref.at[me, 0], seen_ref, small_sem.at[4]),
    ]
    small = [
        pltpu.make_async_copy(tilt_hbm, tilt_ref, small_sem.at[0]),
        pltpu.make_async_copy(table_hbm, table_ref, small_sem.at[1]),
    ]
    loads = [
        pltpu.make_async_copy(waves_ref.at[plane], held.at[plane], in_sem.at[plane])
        for plane in range(planes)
    ]
    for load in small + loads + later:
        load.start()
    for load in small:
        load.wait()
    sub = lax.broadcasted_iota(jnp.int32, (BAND, LANES), 0)
    lane = lax.broadcasted_iota(jnp.int32, (BAND, LANES), 1) - me * planes
    tile = jnp.zeros((BAND, LANES), jnp.float32)
    for beam in range(planes // 2):
        for part in range(2):
            here = lane == 2 * beam + part
            for row in range(4):
                value = table_ref[0, row, beam] if part == 0 else -table_ref[1, row, beam]
                tile = jnp.where(here & (sub == row), value, tile)
            for row in range(2):
                tile = jnp.where(here & (sub == 4 + row), tilt_ref[row, beam].astype(jnp.float32), tile)
    for peer in range(out_ref.shape[0]):
        extra[peer] = tile
    stores = [
        pltpu.make_async_copy(extra, out_ref.at[:, pl.ds(2 * planes * BAND, BAND), :], small_sem.at[2])
    ]
    stores[0].start()
    for plane in range(planes):
        loads[plane].wait()
        for half in range(2):
            store = pltpu.make_async_copy(
                held.at[plane, :, :, pl.ds(half * LANES, LANES)],
                out_ref.at[:, pl.ds((half * planes + plane) * BAND, BAND), :],
                out_sem.at[half * planes + plane],
            )
            store.start()
            stores.append(store)
    for copy in stores + later:
        copy.wait()


def exit_kernel(spots_ref, beside_ref, recv_ref, potential_ref, own_ref, out_ref):
    peers = recv_ref.shape[0]
    extra = recv_ref.shape[1] - BAND
    planes = extra // (2 * BAND)
    count = spots_ref.shape[0]

    table = recv_ref[0, extra:, :]
    for peer in range(1, peers):
        table = table + recv_ref[peer, extra:, :]
    lane = lax.broadcasted_iota(jnp.int32, (BAND, LANES), 1)
    swapped = jnp.where(
        lane % 2 == 0, -pltpu.roll(table, LANES - 1, 1), pltpu.roll(table, 1, 1)
    )
    tilt_row = table[4:5].astype(jnp.int32)
    tilt_col = table[5:6].astype(jnp.int32)

    def coefs(ref):
        row = ref[:, 0:1] - MARGIN
        col = ref[:, 1:2]
        pick = ref[:, 2:3]
        turns = (tilt_row * row + tilt_col * col) & (LANES - 1)
        angle = turns.astype(jnp.float32) * (2.0 * math.pi / LANES)
        u = jnp.zeros((count, LANES), jnp.float32)
        v = jnp.zeros((count, LANES), jnp.float32)
        for n in range(4):
            u = jnp.where(pick == n, table[n : n + 1], u)
            v = jnp.where(pick == n, swapped[n : n + 1], v)
        cosine = jnp.cos(angle)
        sine = jnp.sin(angle)
        return u * cosine + v * sine, v * cosine - u * sine

    weights = split(jnp.concatenate(coefs(spots_ref) + coefs(beside_ref), 0))
    local = potential_ref[...] * SIGMA_SCALE
    trans_re = jnp.cos(local)
    trans_im = jnp.sin(local)
    wide = lax.broadcasted_iota(jnp.int32, (count, LANES), 1)

    for row in range(BAND):
        waves = jnp.concatenate(
            [
                jnp.concatenate(
                    [
                        recv_ref[peer, pl.ds(half * planes * BAND + row, planes, stride=BAND), :]
                        for peer in range(peers)
                    ],
                    0,
                )
                for half in range(2)
            ],
            1,
        )
        summed = exact_dot(weights, split(waves))
        slot = lax.axis_index("beam") * BAND + row
        for side, (ref, target) in enumerate(((spots_ref, own_ref), (beside_ref, out_ref))):
            left = wide >= ref[:, 1:2]
            start = ref[:, 0:1] - MARGIN
            inside = (start <= slot) & (start + LANES > slot)
            keep = inside if side == 0 else ~inside

            def cut(value):
                return jnp.where(left, value[:, :LANES], value[:, LANES:])

            w_re = cut(summed[2 * side * count : (2 * side + 1) * count])
            w_im = cut(summed[(2 * side + 1) * count : (2 * side + 2) * count])
            t_re = cut(trans_re[row : row + 1])
            t_im = cut(trans_im[row : row + 1])
            for part, value in enumerate((t_re * w_re - t_im * w_im, t_re * w_im + t_im * w_re)):
                target[pl.ds(part * BAND + row, count, stride=2 * BAND), :] = jnp.where(
                    keep, value, 0.0
                )


def probe_kernel(recv_ref, dft_ref, seen_ref, misfit_ref, out_ref):
    exit_re = recv_ref[:, :BAND, :].reshape(LANES, LANES)
    exit_im = recv_ref[:, BAND:, :].reshape(LANES, LANES)
    right = [dft_ref[part] for part in range(PARTS)]
    left = [dft_ref[PARTS + part] for part in range(PARTS)]

    def transform(re, im, by_cols, by_rows):
        half = exact_dot(split(jnp.concatenate([re, im], 1)), by_cols)
        full = exact_dot(by_rows, split(jnp.concatenate([half[:, :LANES], half[:, LANES:]], 0)))
        return full[:LANES], full[LANES:]

    far_re, far_im = transform(exit_re, exit_im, right, left)
    misfit = far_re * far_re + far_im * far_im - seen_ref[...]
    misfit_ref[...] = misfit
    back_re, back_im = transform(misfit * far_re, misfit * far_im, left, right)
    piece = SIGMA_SCALE * (exit_re * back_im - exit_im * back_re)
    peers, rows, _ = out_ref.shape
    for peer in range(peers):
        at = peer // SPAN * rows
        out_ref[peer] = piece[at : at + rows]


def place_kernel(spots_ref, recv_ref, core_ref, rim_ref):
    shape = recv_ref.shape[1:]
    slot = lax.broadcasted_iota(jnp.int32, shape, 0) + lax.axis_index("beam") // SPAN * shape[0]
    lane = lax.broadcasted_iota(jnp.int32, shape, 1)
    sums = [jnp.zeros(shape, jnp.float32)] * 4
    for spot in range(recv_ref.shape[0]):
        start = spots_ref[spot : spot + 1, 0:1] - MARGIN
        inside = (slot >= start) & (slot < start + LANES)
        left = lane >= spots_ref[spot : spot + 1, 1:2]
        piece = recv_ref[spot]
        core = jnp.where(inside, piece, 0.0)
        rim = jnp.where(inside, 0.0, piece)
        parts = (jnp.where(left, core, 0.0), jnp.where(left, 0.0, core), jnp.where(left, rim, 0.0), jnp.where(left, 0.0, rim))
        sums = [total + part for total, part in zip(sums, parts)]
    core_ref[:, :LANES], core_ref[:, LANES:], rim_ref[:, :LANES], rim_ref[:, LANES:] = sums


def on_chip(shape):
    return pltpu.VMEM(shape, jnp.float32)


def near(value):
    return pltpu.with_memory_space_constraint(value, VMEM)


def beside_pairs(beams, tiles, outward):
    edge = MARGIN // BAND
    pairs = []
    for band in range(beams):
        step = -1 if band < edge else 1 if band >= beams - edge else 0
        for tile in range(tiles):
            if step and 0 <= tile + step < tiles:
                here, there = band * tiles + tile, band * tiles + tile + step
                pairs.append((here, there) if outward else (there, here))
    return pairs


def shards(
    scattering, potential, row_offset, col_offset, table_index, beam_tilt, coef_table, measured
):
    beam_dev, _, tile_rows, tile_cols = scattering.shape
    beams = lax.axis_size("beam")
    tiles = lax.axis_size("tile")
    planes = 2 * beam_dev
    count = row_offset.shape[0]
    length = measured.shape[-1]
    assert tile_rows == beams * BAND and tile_cols == 2 * LANES and length == LANES
    assert count == beams and beams * planes == LANES
    vmem = pl.BlockSpec(memory_space=VMEM)
    anywhere = pl.BlockSpec(memory_space=pl.ANY)

    spots = jnp.concatenate([row_offset, col_offset, table_index], 1)
    beside = near(lax.ppermute(spots, ("beam", "tile"), beside_pairs(beams, tiles, False)))
    spots = near(spots)

    chunk = 2 * planes * BAND + BAND
    packed, band_potential, seen = pl.pallas_call(
        pack_kernel,
        name="pack",
        in_specs=[anywhere] * 5,
        out_specs=[anywhere, vmem, vmem],
        out_shape=[
            jax.ShapeDtypeStruct((beams, chunk, LANES), jnp.float32),
            on_chip((BAND, tile_cols)),
            on_chip((length, length)),
        ],
        scratch_shapes=[
            pltpu.VMEM((planes, beams, BAND, tile_cols), jnp.float32),
            pltpu.VMEM((beams, BAND, LANES), jnp.float32),
            pltpu.SMEM(beam_tilt.shape, beam_tilt.dtype),
            pltpu.SMEM(coef_table.shape, coef_table.dtype),
            pltpu.SemaphoreType.DMA((planes,)),
            pltpu.SemaphoreType.DMA((2 * planes,)),
            pltpu.SemaphoreType.DMA((5,)),
        ],
    )(beam_tilt, coef_table, scattering.reshape(planes, beams, BAND, tile_cols), potential, measured)
    bands = lax.all_to_all(packed, "beam", 0, 0, tiled=True)

    own, others = pl.pallas_call(
        exit_kernel,
        name="exit",
        in_specs=[vmem] * 4,
        out_specs=[vmem] * 2,
        out_shape=[on_chip((count * 2 * BAND, LANES))] * 2,
    )(spots, beside, near(bands), near(band_potential))
    others = lax.ppermute(others, ("beam", "tile"), beside_pairs(beams, tiles, True))
    exits = lax.all_to_all((own + others).reshape(count, 2 * BAND, LANES), "beam", 0, 0, tiled=True)

    misfit, pieces = pl.pallas_call(
        probe_kernel,
        name="probe",
        in_specs=[vmem] * 3,
        out_specs=[vmem] * 2,
        out_shape=[
            jax.ShapeDtypeStruct((length, length), jnp.float32),
            on_chip((beams, SPAN * BAND, LANES)),
        ],
    )(near(exits), near(jnp.asarray(dft_blocks(length))), near(seen))
    pieces = lax.all_to_all(pieces, "beam", 0, 0, tiled=True)

    band, rims = pl.pallas_call(
        place_kernel,
        name="place",
        in_specs=[vmem] * 2,
        out_specs=[vmem] * 2,
        out_shape=[on_chip((SPAN * BAND, tile_cols))] * 2,
    )(spots, near(pieces))
    band = band + lax.ppermute(rims, ("beam", "tile"), beside_pairs(beams, tiles, False))
    groups = [list(range(at, beams, SPAN)) for at in range(SPAN)]
    core = lax.all_to_all(
        jnp.broadcast_to(band[None], (beams // SPAN, SPAN * BAND, tile_cols)),
        "beam",
        0,
        0,
        axis_index_groups=groups,
        tiled=True,
    )
    return (misfit[None, None], core.reshape(tile_rows, tile_cols))


def solution(mesh):
    in_specs = (
        P("beam", None, "tile", None),
        P("tile", None),
        P(None, "tile"),
        P(None, "tile"),
        P(None, "tile"),
        P(None, "beam"),
        P(None, None, "beam"),
        P(None, "tile", None, None),
    )
    out_specs = (P("beam", "tile", None, None), P("tile", None))
    return jax.shard_map(shards, mesh=mesh, in_specs=in_specs, out_specs=out_specs, check_vma=False)
```

```python
import functools
import math

import jax
import jax.numpy as jnp
import numpy as np
from jax import lax
from jax.experimental import pallas as pl
from jax.experimental.pallas import tpu as pltpu
from jax.sharding import PartitionSpec as P

MARGIN = 32
SIGMA_SCALE = 1.0
LANES = 128
BAND = 8
SPAN = 2

VMEM = pltpu.MemorySpace.VMEM


def dft_blocks(length):
    index = np.arange(length)
    angle = (index[:, None] * index[None, :] % length) * (2.0 * math.pi / length)
    re = np.cos(angle) / math.sqrt(length)
    im = -np.sin(angle) / math.sqrt(length)
    forward = np.block([[re, im], [-im, re]]).astype(np.float32)
    parts = []
    for table in (forward, forward.T):
        high = table.astype(jnp.bfloat16)
        parts += [high, (table - high.astype(np.float32)).astype(jnp.bfloat16)]
    return np.stack(parts)


def split(value):
    high = value.astype(jnp.bfloat16)
    return high, (value - high.astype(jnp.float32)).astype(jnp.bfloat16)


def dot3(left, right):
    lefts = jnp.concatenate([left[0], left[1], left[0]], 1)
    rights = jnp.concatenate([right[0], right[0], right[1]], 0)
    return jnp.dot(lefts, rights, preferred_element_type=jnp.float32)


def pack_kernel(
    tilt_hbm,
    table_hbm,
    waves_ref,
    potential_ref,
    measured_ref,
    out_ref,
    band_ref,
    seen_ref,
    held,
    extra,
    tilt_ref,
    table_ref,
    in_sem,
    out_sem,
    small_sem,
):
    planes = waves_ref.shape[0]
    me = lax.axis_index("beam")
    later = [
        pltpu.make_async_copy(potential_ref.at[pl.ds(me * BAND, BAND)], band_ref, small_sem.at[3]),
        pltpu.make_async_copy(measured_ref.at[me, 0], seen_ref, small_sem.at[4]),
    ]
    small = [
        pltpu.make_async_copy(tilt_hbm, tilt_ref, small_sem.at[0]),
        pltpu.make_async_copy(table_hbm, table_ref, small_sem.at[1]),
    ]
    loads = [
        pltpu.make_async_copy(waves_ref.at[plane], held.at[plane], in_sem.at[plane])
        for plane in range(planes)
    ]
    for load in small + loads + later:
        load.start()
    for load in small:
        load.wait()
    sub = lax.broadcasted_iota(jnp.int32, (BAND, LANES), 0)
    lane = lax.broadcasted_iota(jnp.int32, (BAND, LANES), 1) - me * planes
    tile = jnp.zeros((BAND, LANES), jnp.float32)
    for beam in range(planes // 2):
        for part in range(2):
            here = lane == 2 * beam + part
            for row in range(4):
                value = table_ref[0, row, beam] if part == 0 else -table_ref[1, row, beam]
                tile = jnp.where(here & (sub == row), value, tile)
            for row in range(2):
                tile = jnp.where(here & (sub == 4 + row), tilt_ref[row, beam].astype(jnp.float32), tile)
    for peer in range(out_ref.shape[0]):
        extra[peer] = tile
    stores = [
        pltpu.make_async_copy(extra, out_ref.at[:, pl.ds(2 * planes * BAND, BAND), :], small_sem.at[2])
    ]
    stores[0].start()
    for plane in range(planes):
        loads[plane].wait()
        for half in range(2):
            store = pltpu.make_async_copy(
                held.at[plane, :, :, pl.ds(half * LANES, LANES)],
                out_ref.at[:, pl.ds((half * planes + plane) * BAND, BAND), :],
                out_sem.at[half * planes + plane],
            )
            store.start()
            stores.append(store)
    for copy in stores + later:
        copy.wait()


def exit_kernel(own, spots_ref, recv_ref, potential_ref, out_ref):
    peers = recv_ref.shape[0]
    extra = recv_ref.shape[1] - BAND
    planes = extra // (2 * BAND)
    count = spots_ref.shape[0]

    table = recv_ref[0, extra:, :]
    for peer in range(1, peers):
        table = table + recv_ref[peer, extra:, :]
    lane = lax.broadcasted_iota(jnp.int32, (BAND, LANES), 1)
    swapped = jnp.where(
        lane % 2 == 0, -pltpu.roll(table, LANES - 1, 1), pltpu.roll(table, 1, 1)
    )
    tilt_row = table[4:5].astype(jnp.int32)
    tilt_col = table[5:6].astype(jnp.int32)

    def coefs(ref):
        row = ref[:, 0:1] - MARGIN
        col = ref[:, 1:2]
        pick = ref[:, 2:3]
        turns = (tilt_row * row + tilt_col * col) & (LANES - 1)
        angle = turns.astype(jnp.float32) * (2.0 * math.pi / LANES)
        u = jnp.zeros((count, LANES), jnp.float32)
        v = jnp.zeros((count, LANES), jnp.float32)
        for n in range(4):
            u = jnp.where(pick == n, table[n : n + 1], u)
            v = jnp.where(pick == n, swapped[n : n + 1], v)
        cosine = jnp.cos(angle)
        sine = jnp.sin(angle)
        return u * cosine + v * sine, v * cosine - u * sine

    weights = split(jnp.concatenate(coefs(spots_ref), 0))
    local = potential_ref[...] * SIGMA_SCALE
    trans_re = jnp.cos(local)
    trans_im = jnp.sin(local)
    wide = lax.broadcasted_iota(jnp.int32, (count, LANES), 1)

    for row in range(BAND):
        waves = jnp.concatenate(
            [
                jnp.concatenate(
                    [
                        recv_ref[peer, pl.ds(half * planes * BAND + row, planes, stride=BAND), :]
                        for peer in range(peers)
                    ],
                    0,
                )
                for half in range(2)
            ],
            1,
        )
        summed = dot3(weights, split(waves))
        slot = lax.axis_index("beam") * BAND + row
        left = wide >= spots_ref[:, 1:2]
        start = spots_ref[:, 0:1] - MARGIN
        inside = (start <= slot) & (start + LANES > slot)
        keep = inside if own else ~inside

        def cut(value):
            return jnp.where(left, value[:, :LANES], value[:, LANES:])

        w_re = cut(summed[:count])
        w_im = cut(summed[count:])
        t_re = cut(trans_re[row : row + 1])
        t_im = cut(trans_im[row : row + 1])
        for part, value in enumerate((t_re * w_re - t_im * w_im, t_re * w_im + t_im * w_re)):
            out_ref[pl.ds(part * BAND + row, count, stride=2 * BAND), :] = jnp.where(keep, value, 0.0)


def probe_kernel(recv_ref, dft_ref, seen_ref, misfit_ref, out_ref):
    exit_re = recv_ref[:, :BAND, :].reshape(LANES, LANES)
    exit_im = recv_ref[:, BAND:, :].reshape(LANES, LANES)
    right = (dft_ref[0], dft_ref[1])
    left = (dft_ref[2], dft_ref[3])

    def transform(re, im, by_cols, by_rows):
        half = dot3(split(jnp.concatenate([re, im], 1)), by_cols)
        full = dot3(by_rows, split(jnp.concatenate([half[:, :LANES], half[:, LANES:]], 0)))
        return full[:LANES], full[LANES:]

    far_re, far_im = transform(exit_re, exit_im, right, left)
    misfit = far_re * far_re + far_im * far_im - seen_ref[...]
    misfit_ref[...] = misfit
    back_re, back_im = transform(misfit * far_re, misfit * far_im, left, right)
    piece = SIGMA_SCALE * (exit_re * back_im - exit_im * back_re)
    peers, rows, _ = out_ref.shape
    for peer in range(peers):
        at = peer // SPAN * rows
        out_ref[peer] = piece[at : at + rows]


def place_kernel(spots_ref, recv_ref, core_ref, rim_ref):
    shape = recv_ref.shape[1:]
    slot = lax.broadcasted_iota(jnp.int32, shape, 0) + lax.axis_index("beam") // SPAN * shape[0]
    lane = lax.broadcasted_iota(jnp.int32, shape, 1)
    sums = [jnp.zeros(shape, jnp.float32)] * 4
    for spot in range(recv_ref.shape[0]):
        start = spots_ref[spot : spot + 1, 0:1] - MARGIN
        inside = (slot >= start) & (slot < start + LANES)
        left = lane >= spots_ref[spot : spot + 1, 1:2]
        piece = recv_ref[spot]
        core = jnp.where(inside, piece, 0.0)
        rim = jnp.where(inside, 0.0, piece)
        parts = (jnp.where(left, core, 0.0), jnp.where(left, 0.0, core), jnp.where(left, rim, 0.0), jnp.where(left, 0.0, rim))
        sums = [total + part for total, part in zip(sums, parts)]
    core_ref[:, :LANES], core_ref[:, LANES:], rim_ref[:, :LANES], rim_ref[:, LANES:] = sums


def on_chip(shape):
    return pltpu.VMEM(shape, jnp.float32)


def near(value):
    return pltpu.with_memory_space_constraint(value, VMEM)


def beside_pairs(beams, tiles, outward):
    edge = MARGIN // BAND
    pairs = []
    for band in range(beams):
        step = -1 if band < edge else 1 if band >= beams - edge else 0
        for tile in range(tiles):
            if step and 0 <= tile + step < tiles:
                here, there = band * tiles + tile, band * tiles + tile + step
                pairs.append((here, there) if outward else (there, here))
    return pairs


def shards(
    scattering, potential, row_offset, col_offset, table_index, beam_tilt, coef_table, measured
):
    beam_dev, _, tile_rows, tile_cols = scattering.shape
    beams = lax.axis_size("beam")
    tiles = lax.axis_size("tile")
    planes = 2 * beam_dev
    count = row_offset.shape[0]
    length = measured.shape[-1]
    assert tile_rows == beams * BAND and tile_cols == 2 * LANES and length == LANES
    assert count == beams and beams * planes == LANES
    vmem = pl.BlockSpec(memory_space=VMEM)
    anywhere = pl.BlockSpec(memory_space=pl.ANY)

    spots = jnp.concatenate([row_offset, col_offset, table_index], 1)
    beside = near(lax.ppermute(spots, ("beam", "tile"), beside_pairs(beams, tiles, False)))
    spots = near(spots)

    chunk = 2 * planes * BAND + BAND
    packed, band_potential, seen = pl.pallas_call(
        pack_kernel,
        name="pack",
        in_specs=[anywhere] * 5,
        out_specs=[anywhere, vmem, vmem],
        out_shape=[
            jax.ShapeDtypeStruct((beams, chunk, LANES), jnp.float32),
            on_chip((BAND, tile_cols)),
            on_chip((length, length)),
        ],
        scratch_shapes=[
            pltpu.VMEM((planes, beams, BAND, tile_cols), jnp.float32),
            pltpu.VMEM((beams, BAND, LANES), jnp.float32),
            pltpu.SMEM(beam_tilt.shape, beam_tilt.dtype),
            pltpu.SMEM(coef_table.shape, coef_table.dtype),
            pltpu.SemaphoreType.DMA((planes,)),
            pltpu.SemaphoreType.DMA((2 * planes,)),
            pltpu.SemaphoreType.DMA((5,)),
        ],
    )(beam_tilt, coef_table, scattering.reshape(planes, beams, BAND, tile_cols), potential, measured)
    bands = lax.all_to_all(packed, "beam", 0, 0, tiled=True)

    bands = near(bands)
    band_potential = near(band_potential)

    def exits_of(positions, own):
        return pl.pallas_call(
            functools.partial(exit_kernel, own),
            name="exit_own" if own else "exit_beside",
            in_specs=[vmem] * 3,
            out_specs=vmem,
            out_shape=on_chip((count * 2 * BAND, LANES)),
        )(positions, bands, band_potential)

    others = lax.ppermute(
        exits_of(beside, False), ("beam", "tile"), beside_pairs(beams, tiles, True)
    )
    own = exits_of(spots, True)
    exits = lax.all_to_all((own + others).reshape(count, 2 * BAND, LANES), "beam", 0, 0, tiled=True)

    misfit, pieces = pl.pallas_call(
        probe_kernel,
        name="probe",
        in_specs=[vmem] * 3,
        out_specs=[vmem] * 2,
        out_shape=[
            jax.ShapeDtypeStruct((length, length), jnp.float32),
            on_chip((beams, SPAN * BAND, LANES)),
        ],
    )(near(exits), near(jnp.asarray(dft_blocks(length))), near(seen))
    pieces = lax.all_to_all(pieces, "beam", 0, 0, tiled=True)

    band, rims = pl.pallas_call(
        place_kernel,
        name="place",
        in_specs=[vmem] * 2,
        out_specs=[vmem] * 2,
        out_shape=[on_chip((SPAN * BAND, tile_cols))] * 2,
    )(spots, near(pieces))
    band = band + lax.ppermute(rims, ("beam", "tile"), beside_pairs(beams, tiles, False))
    groups = [list(range(at, beams, SPAN)) for at in range(SPAN)]
    core = lax.all_to_all(
        jnp.broadcast_to(band[None], (beams // SPAN, SPAN * BAND, tile_cols)),
        "beam",
        0,
        0,
        axis_index_groups=groups,
        tiled=True,
    )
    return (misfit[None, None], core.reshape(tile_rows, tile_cols))


def solution(mesh):
    in_specs = (
        P("beam", None, "tile", None),
        P("tile", None),
        P(None, "tile"),
        P(None, "tile"),
        P(None, "tile"),
        P(None, "beam"),
        P(None, None, "beam"),
        P(None, "tile", None, None),
    )
    out_specs = (P("beam", "tile", None, None), P("tile", None))
    return jax.shard_map(shards, mesh=mesh, in_specs=in_specs, out_specs=out_specs, check_vma=False)
```
